32 devices in a mesh: parts: 2 (over y), tm: 4 (over z), axial: 2 (over x), chan: 2 (over core).
Axes of the slice: x: 2, y: 2, z: 4, core: 2. Of those that a mesh axis runs over, the one named last changes fastest.
Arguments:
- frames_in: bfloat16 [48, 8, 64, 128], P(('parts', 'tm'), 'axial'), parts along dimension 0, may hold values from -6 to 6
- spatial_weight: bfloat16 [6, 3, 64, 144], P('parts', None, None, 'chan'), parts along dimension 0, may hold values from -0.25 to 0.25
- temporal_weight: bfloat16 [6, 144, 64], P('parts', 'chan'), parts along dimension 0, may hold values from -0.3125 to 0.3125
- upstream: bfloat16 [48, 8, 64, 128], P(('parts', 'tm'), 'axial'), parts along dimension 0, may hold values from -6 to 6
Outputs:
- output: bfloat16 [48, 8, 64, 128], P(('parts', 'tm'), 'axial', 'chan'), parts along dimension 0
- input_grad: bfloat16 [48, 8, 64, 128], P(('parts', 'tm'), 'axial', 'chan'), parts along dimension 0
- spatial_grad: float32 [6, 3, 64, 144], P('parts', None, None, 'chan'), parts along dimension 0
- temporal_grad: float32 [6, 144, 64], P('parts', 'chan'), parts along dimension 0
The draws below stay inside these ranges and needn't reach their ends.
There are 2 independent parts, one for each index of `parts`. The reference program is written for one: setup_inputs(seed, part) draws one part's arguments, and reference() takes and returns one part's arrays. A program takes and returns all parts, laid end to end along the dimension named above; each array names one. Nothing has to cross between parts.
All inputs are finite; a program needn't handle non-finite values.
Results may differ from the reference program's by a relative error of at most 0.009.
Values may be sent and summed in bfloat16 or wider, within the bound.
A program may use at most 64 MiB of HBM per device.

```python
import math
import jax
import jax.numpy as jnp
from jax import lax

CH = 64
MID = 144
WD = 128
FRAMES = 24
ROWS = 8


def level_of(rng, dims, pieces, smallest, high):
    gain = 1.0
    for position, blocks in pieces:
        draws = jax.random.uniform(jax.random.fold_in(jax.random.fold_in(rng, 6), position), (blocks,), jnp.float32, smallest / len(pieces), high / len(pieces))
        gain = gain * jnp.repeat(jnp.exp(draws), dims[position] // blocks).reshape((-1,) + (1,) * (len(dims) - 1 - position))
    return gain


def noise(rng, extent, width, limit, shards=(), kind=jnp.bfloat16):
    entries = width * jax.random.normal(rng, extent, jnp.float32)
    if shards:
        entries = entries * level_of(rng, extent, shards, -0.22, 0.18)
    return jnp.clip(entries, -limit, limit).astype(kind)


def setup_inputs(seed: int = 0, part: int = 0) -> dict:
    arg_keys = jax.random.split(jax.random.key(seed), 5)
    part_keys = jax.random.split(jax.random.fold_in(arg_keys[4], part), 5)
    frames_in = noise(part_keys[0], (FRAMES, ROWS, CH, WD), 1.0, 6.0, ((0, 4), (1, 2)))
    spatial_weight = noise(part_keys[1], (3, 3, CH, MID), (9 * CH) ** -0.5, 0.25, ((3, 2),))
    temporal_weight = noise(part_keys[2], (3, MID, CH), (3 * MID) ** -0.5, 0.3125, ((1, 2),))
    upstream = noise(part_keys[3], (FRAMES, ROWS, CH, WD), 1.0, 6.0, ((0, 4), (1, 2)))
    return {"frames_in": frames_in, "spatial_weight": spatial_weight, "temporal_weight": temporal_weight, "upstream": upstream}


def conv_same(lhs_arr, rhs_arr, specs):
    return lax.conv_general_dilated(lhs_arr.astype(jnp.float32), rhs_arr.astype(jnp.float32), (1, 1), ((1, 1), (1, 1)), dimension_numbers=specs, preferred_element_type=jnp.float32)

def reference(frames_in, spatial_weight, temporal_weight, upstream):
    frame_total, row_total, channels, width_total = frames_in.shape
    factor = 1.0 / math.sqrt(frame_total * row_total * width_total)
    preact = conv_same(frames_in, spatial_weight, ('NHCW', 'HWIO', 'NHCW'))
    hidden = lax.optimization_barrier(jax.nn.silu(preact).astype(jnp.bfloat16))
    hidden_wide = hidden.astype(jnp.float32)
    upstream_wide = upstream.astype(jnp.float32)
    weight_wide = temporal_weight.astype(jnp.float32)
    summed = jnp.zeros(frames_in.shape, jnp.float32)
    grad_act = jnp.zeros(preact.shape, jnp.float32)
    temporal_list = []
    for offset in range(3):
        moved = jnp.roll(hidden_wide, 1 - offset, axis=0)
        summed = summed + jnp.einsum('fhmw,mc->fhcw', moved, weight_wide[offset])
        grad_act = grad_act + jnp.einsum('fhcw,mc->fhmw', jnp.roll(upstream_wide, offset - 1, axis=0), weight_wide[offset])
        temporal_list.append(jnp.einsum('fhmw,fhcw->mc', moved, upstream_wide))
    output = summed.astype(jnp.bfloat16)
    temporal_grad = jnp.stack(temporal_list) * factor
    sigma = jax.nn.sigmoid(preact)
    grad_pre = lax.optimization_barrier((grad_act * sigma * (1.0 + preact * (1.0 - sigma))).astype(jnp.bfloat16))
    grad_wide = grad_pre.astype(jnp.float32)
    padded = jnp.pad(frames_in.astype(jnp.float32), ((0, 0), (1, 1), (0, 0), (1, 1)))
    spatial_rows = []
    for i in range(3):
        spatial_rows.append(jnp.stack([jnp.einsum('fhcw,fhmw->cm', padded[:, i:i + row_total, :, j:j + width_total], grad_wide) for j in range(3)]))
    spatial_grad = jnp.stack(spatial_rows) * factor
    input_grad = conv_same(grad_wide, spatial_weight[::-1, ::-1], ('NHCW', 'HWOI', 'NHCW')).astype(jnp.bfloat16)
    return (output, input_grad, spatial_grad, temporal_grad)
```

```python
import functools
import math

import jax
import jax.numpy as jnp
from jax import lax
from jax.experimental import pallas as pl
from jax.experimental.pallas import tpu as pltpu
from jax.sharding import PartitionSpec as P

MESH = pl.DeviceIdType.MESH
F32 = jnp.float32
BF16 = jnp.bfloat16
NT = (((1,), (1,)), ((), ()))


def mm(a, b):
    return jnp.dot(a, b, preferred_element_type=F32)


def mm_nt(a, b):
    return lax.dot_general(a, b, NT, preferred_element_type=F32)


def shifted(block, step):
    if step == 0:
        return block
    width = block.shape[1]
    lane = lax.broadcasted_iota(jnp.int32, block.shape, 1)
    edge = 0 if step > 0 else width - 1
    return jnp.where(lane == edge, 0.0, pltpu.roll(block, step % width, axis=1))


def kernel(
    dims, x, u, wf, wi, tg, to, out, ig, sg, tgrad,
    xh, uh, hid, gs, gh, ga, o_own, o_send, o_recv, i_own, i_send, i_recv,
    acc, rs_send, rs_recv, red,
    xs_sem, xr_sem, us_sem, ur_sem, hs_sem, hr_sem, gs_sem, gr_sem,
    os_sem, or_sem, is_sem, ir_sem, rss_sem, rsr_sem, ags_sem, agr_sem,
):
    F, H, C, W, M, MP, T, A, factor, owners, rp = dims
    CS = C // 2
    n = T * A
    t, a, ch = lax.axis_index("tm"), lax.axis_index("axial"), lax.axis_index("chan")
    oc = 1 - ch
    g = t * A + a
    prev_t, next_t = lax.rem(t + T - 1, T), lax.rem(t + 1, T)

    def peer(d):
        p = lax.rem(g + d, n)
        return p, {"tm": p // A, "axial": lax.rem(p, A)}

    barrier = pltpu.get_barrier_semaphore()
    for d in range(1, n):
        pl.semaphore_signal(barrier, inc=1, device_id=peer(d)[1], device_id_type=MESH)
    pl.semaphore_signal(barrier, inc=1, device_id={"chan": oc}, device_id_type=MESH)
    acc[...] = jnp.zeros_like(acc)
    pl.semaphore_wait(barrier, n)

    def remote(src, dst, s, r, dev):
        return pltpu.make_async_remote_copy(
            src_ref=src, dst_ref=dst, send_sem=s, recv_sem=r, device_id=dev, device_id_type=MESH
        )

    up_dev = {"axial": jnp.maximum(a - 1, 0)}
    down_dev = {"axial": jnp.minimum(a + 1, A - 1)}
    has_up, has_down = a > 0, a < A - 1
    x_down = remote(x.at[:, H - 1], xh.at[0], xs_sem.at[0], xr_sem.at[0], down_dev)
    x_up = remote(x.at[:, 0], xh.at[1], xs_sem.at[1], xr_sem.at[1], up_dev)
    u_next = remote(u.at[F - 1], uh.at[0], us_sem.at[0], ur_sem.at[0], {"tm": next_t})
    u_prev = remote(u.at[0], uh.at[1], us_sem.at[1], ur_sem.at[1], {"tm": prev_t})

    @pl.when(has_down)
    def _():
        x_down.start()

    @pl.when(has_up)
    def _():
        x_up.start()

    u_next.start()
    u_prev.start()

    def lanes(rows):
        return jnp.concatenate(rows, axis=1)

    def u_at(f, h):
        if f < 0:
            return uh[0, h]
        if f >= F:
            return uh[1, h]
        return u[f, h]

    def u_stack(f):
        return lanes([jnp.concatenate([u_at(f - 1, h), u_at(f, h), u_at(f + 1, h)], axis=0) for h in range(H)])

    for f in range(1, F - 1):
        ga[f] = mm(tg[...], u_stack(f))

    @pl.when(jnp.logical_not(has_up))
    def _():
        xh[0] = jnp.zeros((F, C, W), BF16)
        gh[0] = jnp.zeros((F, MP, W), BF16)

    @pl.when(jnp.logical_not(has_down))
    def _():
        xh[1] = jnp.zeros((F, C, W), BF16)
        gh[1] = jnp.zeros((F, MP, W), BF16)

    u_next.wait_recv()
    u_prev.wait_recv()
    for f in (0, F - 1):
        ga[f] = mm(tg[...], u_stack(f))

    @pl.when(has_up)
    def _():
        x_down.wait_recv()

    @pl.when(has_down)
    def _():
        x_up.wait_recv()

    h_next = remote(hid.at[F], hid.at[0], hs_sem.at[0], hr_sem.at[0], {"tm": next_t})
    h_prev = remote(hid.at[1], hid.at[F + 1], hs_sem.at[1], hr_sem.at[1], {"tm": prev_t})

    def g_down(f):
        return remote(gs.at[f, H - 1, 1], gh.at[0, f], gs_sem.at[0, f], gr_sem.at[0, f], down_dev)

    def g_up(f):
        return remote(gs.at[f, 0, 1], gh.at[1, f], gs_sem.at[1, f], gr_sem.at[1, f], up_dev)

    for f in [0, F - 1] + list(range(1, F - 1)):
        rows = [xh[0, f]] + [x[f, h] for h in range(H)] + [xh[1, f]]
        xst = lanes([jnp.concatenate(rows[h : h + 3], axis=0) for h in range(H)])
        y = mm(wf[...], xst)
        hs, gsh = [], []
        for h in range(H):
            sl = slice(h * W, (h + 1) * W)
            pre = (
                shifted(y[0:MP, sl], 1) + y[MP : 2 * MP, sl] + shifted(y[2 * MP :, sl], -1)
            )
            sig = 1.0 / (1.0 + jnp.exp(-pre))
            hv = (pre * sig).astype(BF16)
            hid[f + 1, h] = hv
            hs.append(hv)
            gv = ga[f, :, sl] * sig * (1.0 + pre * (1.0 - sig))
            trio = [shifted(gv, j - 1).astype(BF16) for j in range(3)]
            for j in range(3):
                gs[f, h, j] = trio[j]
            gsh.append(jnp.concatenate(trio, axis=0))
        if f == 0:
            h_prev.start()
        if f == F - 1:
            h_next.start()

        @pl.when(has_down)
        def _():
            g_down(f).start()

        @pl.when(has_up)
        def _():
            g_up(f).start()

        acc[:, 0 : 3 * MP] += mm_nt(xst, lanes(gsh))
        acc[:, T0 : T0 + MP] += mm_nt(u_stack(f), lanes(hs))

    for p in range(owners):
        rs_send[p] = (acc[p * rp : (p + 1) * rp] * factor).astype(BF16)

    def rs_copy(d):
        p, dev = peer(d)
        return remote(rs_send.at[lax.rem(p, owners)], rs_recv.at[d - 1], rss_sem.at[d - 1], rsr_sem.at[d - 1], dev)

    def guarded(cond, do):
        if owners == n:
            do()
        else:
            pl.when(cond)(do)

    for d in range(1, n):
        guarded(peer(d)[0] < owners, lambda: rs_copy(d).start())

    own_rows = pl.ds(pl.multiple_of(ch * CS, CS), CS)
    far_rows = pl.ds(pl.multiple_of(oc * CS, CS), CS)
    to2 = jnp.concatenate([to[own_rows, :], to[far_rows, :]], axis=0)

    def o_copy(f):
        return remote(o_send.at[f], o_recv.at[f], os_sem.at[f], or_sem.at[f], {"chan": oc})

    def i_copy(f):
        return remote(i_send.at[f], i_recv.at[f], is_sem.at[f], ir_sem.at[f], {"chan": oc})

    for f in list(range(1, F - 1)) + [0, F - 1]:
        if f == 0:
            h_next.wait_recv()
        if f == F - 1:
            h_prev.wait_recv()
        st = lanes([jnp.concatenate([hid[f + k, h] for k in range(3)], axis=0) for h in range(H)])
        y = mm(to2, st)
        for h in range(H):
            sl = slice(h * W, (h + 1) * W)
            o_own[f, h] = y[:CS, sl]
            o_send[f, h] = y[CS:, sl].astype(BF16)
        o_copy(f).start()

    def ag_copy(d):
        _, dev = peer(d)
        mine = red.at[lax.rem(g, owners)]
        return remote(mine, mine, ags_sem.at[d - 1], agr_sem.at[d - 1], dev)

    def reduce_piece():
        total = acc[pl.ds(pl.multiple_of(lax.rem(g, owners) * rp, 8), rp), :] * factor
        for d in range(1, n):
            rs_copy(d).wait_recv()
            total = total + rs_recv[d - 1].astype(F32)
        red[lax.rem(g, owners)] = total.astype(BF16)
        for d in range(1, n):
            ag_copy(d).start()

    wi2 = jnp.concatenate(
        [wi[i, own_rows, :] for i in range(3)] + [wi[i, far_rows, :] for i in range(3)], axis=0
    )
    for f in range(F):
        if f == F // 2:
            guarded(g < owners, reduce_piece)

        @pl.when(has_up)
        def _():
            g_down(f).wait_recv()

        @pl.when(has_down)
        def _():
            g_up(f).wait_recv()

        halo = []
        for side in range(2):
            gv = gh[side, f].astype(F32)
            halo.append(jnp.concatenate([shifted(gv, j - 1).astype(BF16) for j in range(3)], axis=0))
        body = [jnp.concatenate([gs[f, h, j] for j in range(3)], axis=0) for h in range(H)]
        y = mm(wi2, lanes([halo[0]] + body + [halo[1]]))
        for h in range(H):
            def part(base):
                s = None
                for i in range(3):
                    e = h + 2 - i
                    v = y[base + i * CS : base + (i + 1) * CS, e * W : (e + 1) * W]
                    s = v if s is None else s + v
                return s

            i_own[f, h] = part(0)
            i_send[f, h] = part(3 * CS).astype(BF16)
        i_copy(f).start()

    for f in range(F):
        o_copy(f).wait_recv()
        out[f] = (o_own[f] + o_recv[f].astype(F32)).astype(BF16)
    for f in range(F):
        i_copy(f).wait_recv()
        ig[f] = (i_own[f] + i_recv[f].astype(F32)).astype(BF16)

    for d in range(1, n):
        src = lax.rem(g + n - d, n)

        def arrive():
            dst = red.at[lax.rem(src, owners)]
            remote(dst, dst, ags_sem.at[d - 1], agr_sem.at[d - 1], peer(n - d)[1]).wait_recv()

        guarded(src < owners, arrive)
    total = jnp.concatenate([red[p].astype(F32) for p in range(owners)], axis=0)
    for i in range(3):
        for j in range(3):
            sg[i, j] = total[i * C : (i + 1) * C, j * MP : j * MP + M]
    for k in range(3):
        tgrad[2 - k] = jnp.transpose(total[k * C : (k + 1) * C, T0 : T0 + 128])[:M]

    @pl.when(has_down)
    def _():
        x_down.wait_send()
        for f in range(F):
            g_down(f).wait_send()

    @pl.when(has_up)
    def _():
        x_up.wait_send()
        for f in range(F):
            g_up(f).wait_send()

    u_next.wait_send()
    u_prev.wait_send()
    h_next.wait_send()
    h_prev.wait_send()
    for f in range(F):
        o_copy(f).wait_send()
        i_copy(f).wait_send()
    for d in range(1, n):
        guarded(peer(d)[0] < owners, lambda: rs_copy(d).wait_send())
        guarded(g < owners, lambda: ag_copy(d).wait_send())


T0 = 256


def shards(x, sw, tw, u):
    F, H, C, W = x.shape
    M = tw.shape[1]
    MP = -(-M // 16) * 16
    T, A = lax.axis_size("tm"), lax.axis_size("axial")
    n = T * A
    factor = 1.0 / math.sqrt(F * T * H * A * W)
    R, L = 3 * C, T0 + 128
    rp = next(r for r in range(8, R + 1, 8) if R % r == 0 and R // r <= n)
    owners = R // rp
    CS = C // 2
    swp = jnp.pad(sw, ((0, 0), (0, 0), (0, 0), (0, MP - M)))
    twp = jnp.pad(tw, ((0, 0), (0, MP - M), (0, 0)))
    wf = jnp.transpose(swp, (1, 3, 0, 2)).reshape(3 * MP, 3 * C)
    wi = jnp.transpose(swp, (0, 2, 1, 3)).reshape(3, C, 3 * MP)
    tg = jnp.transpose(twp[::-1], (1, 0, 2)).reshape(MP, 3 * C)
    to = jnp.transpose(twp, (2, 0, 1)).reshape(C, 3 * MP)
    vm = pl.BlockSpec(memory_space=pltpu.VMEM)
    dma = pltpu.SemaphoreType.DMA
    return pl.pallas_call(
        functools.partial(kernel, (F, H, C, W, M, MP, T, A, factor, owners, rp)),
        out_shape=(
            jax.ShapeDtypeStruct((F, H, CS, W), BF16),
            jax.ShapeDtypeStruct((F, H, CS, W), BF16),
            jax.ShapeDtypeStruct((3, 3, C, M), F32),
            jax.ShapeDtypeStruct((3, M, C), F32),
        ),
        in_specs=[vm] * 6,
        out_specs=[vm] * 4,
        scratch_shapes=[
            pltpu.VMEM((2, F, C, W), BF16),
            pltpu.VMEM((2, H, C, W), BF16),
            pltpu.VMEM((F + 2, H, MP, W), BF16),
            pltpu.VMEM((F, H, 3, MP, W), BF16),
            pltpu.VMEM((2, F, MP, W), BF16),
            pltpu.VMEM((F, MP, H * W), F32),
            pltpu.VMEM((F, H, CS, W), F32),
            pltpu.VMEM((F, H, CS, W), BF16),
            pltpu.VMEM((F, H, CS, W), BF16),
            pltpu.VMEM((F, H, CS, W), F32),
            pltpu.VMEM((F, H, CS, W), BF16),
            pltpu.VMEM((F, H, CS, W), BF16),
            pltpu.VMEM((R, L), F32),
            pltpu.VMEM((owners, rp, L), BF16),
            pltpu.VMEM((n - 1, rp, L), BF16),
            pltpu.VMEM((owners, rp, L), BF16),
            dma((2,)), dma((2,)), dma((2,)), dma((2,)), dma((2,)), dma((2,)),
            dma((2, F)), dma((2, F)),
            dma((F,)), dma((F,)), dma((F,)), dma((F,)),
            dma((n - 1,)), dma((n - 1,)), dma((n - 1,)), dma((n - 1,)),
        ],
        compiler_params=pltpu.CompilerParams(collective_id=0, has_side_effects=True),
    )(x, u, wf, wi, tg, to)


def solution(mesh):
    placed = (
        P(("parts", "tm"), "axial", None, None),
        P("parts", None, None, "chan"),
        P("parts", "chan", None),
        P(("parts", "tm"), "axial", None, None),
    )
    return jax.shard_map(
        shards,
        mesh=mesh,
        in_specs=placed,
        out_specs=(
            P(("parts", "tm"), "axial", "chan", None),
            P(("parts", "tm"), "axial", "chan", None),
            P("parts", None, None, "chan"),
            P("parts", "chan", None),
        ),
        check_vma=False,
    )
```

```python
import functools
import math

import jax
import jax.numpy as jnp
from jax import lax
from jax.experimental import pallas as pl
from jax.experimental.pallas import tpu as pltpu
from jax.sharding import PartitionSpec as P

MESH = pl.DeviceIdType.MESH
F32 = jnp.float32
BF16 = jnp.bfloat16
NT = (((1,), (1,)), ((), ()))


def mm(a, b):
    return jnp.dot(a, b, preferred_element_type=F32)


def mm_nt(a, b):
    return lax.dot_general(a, b, NT, preferred_element_type=F32)


def shifted(block, step):
    if step == 0:
        return block
    width = block.shape[1]
    lane = lax.broadcasted_iota(jnp.int32, block.shape, 1)
    edge = 0 if step > 0 else width - 1
    return jnp.where(lane == edge, 0.0, pltpu.roll(block, step % width, axis=1))


def kernel(
    dims, x, u, sw, tw, out, ig, sg, tgrad,
    wf, wi, tg, to,
    xh, uh, hid, gs, gh, ga, o_own, o_send, o_recv, i_own, i_send, i_recv,
    acc, rs_send, rs_recv, red,
    xs_sem, xr_sem, us_sem, ur_sem, hs_sem, hr_sem, gs_sem, gr_sem,
    os_sem, or_sem, is_sem, ir_sem, rss_sem, rsr_sem, ags_sem, agr_sem,
):
    F, H, C, W, M, MP, T, A, factor, owners, rp = dims
    CS = C // 2
    n = T * A
    t, a, ch = lax.axis_index("tm"), lax.axis_index("axial"), lax.axis_index("chan")
    oc = 1 - ch
    g = t * A + a
    prev_t, next_t = lax.rem(t + T - 1, T), lax.rem(t + 1, T)

    def peer(d):
        p = lax.rem(g + d, n)
        return p, {"tm": p // A, "axial": lax.rem(p, A)}

    def lanes(rows):
        return jnp.concatenate(rows, axis=1)

    def u_at(f, h):
        if f < 0:
            return uh[0, h]
        if f >= F:
            return uh[1, h]
        return u[f, h]

    def u_stack(f):
        return lanes([jnp.concatenate([u_at(f - 1, h), u_at(f, h), u_at(f + 1, h)], axis=0) for h in range(H)])

    def ga_inner():
        for f in range(1, F - 1):
            ga[f] = mm(tg[...], u_stack(f))

    barrier = pltpu.get_barrier_semaphore()
    for d in range(1, n):
        pl.semaphore_signal(barrier, inc=1, device_id=peer(d)[1], device_id_type=MESH)
    pl.semaphore_signal(barrier, inc=1, device_id={"chan": oc}, device_id_type=MESH)
    acc[...] = jnp.zeros_like(acc)

    def widen(parts):
        zero = jnp.zeros((parts[0].shape[0], MP - M), F32)
        return jnp.concatenate([v for p in parts for v in (p.astype(F32), zero)], axis=1)

    tcol = [widen([tw[k]]) for k in range(3)]
    tg[...] = jnp.transpose(jnp.concatenate(tcol[::-1], axis=0)).astype(BF16)
    to[...] = jnp.concatenate(tcol, axis=1).astype(BF16)
    ga_inner()
    wide = jnp.concatenate([widen([sw[i, j] for j in range(3)]) for i in range(3)], axis=0)
    wf[...] = jnp.transpose(wide).astype(BF16)
    for i in range(3):
        wi[i] = wide[i * C : (i + 1) * C].astype(BF16)
    pl.semaphore_wait(barrier, n)

    def remote(src, dst, s, r, dev):
        return pltpu.make_async_remote_copy(
            src_ref=src, dst_ref=dst, send_sem=s, recv_sem=r, device_id=dev, device_id_type=MESH
        )

    up_dev = {"axial": jnp.maximum(a - 1, 0)}
    down_dev = {"axial": jnp.minimum(a + 1, A - 1)}
    has_up, has_down = a > 0, a < A - 1
    def x_down(f):
        return remote(x.at[f, H - 1], xh.at[0, f], xs_sem.at[0, f], xr_sem.at[0, f], down_dev)

    def x_up(f):
        return remote(x.at[f, 0], xh.at[1, f], xs_sem.at[1, f], xr_sem.at[1, f], up_dev)

    order = [0, F - 1] + list(range(1, F - 1))
    u_next = remote(u.at[F - 1], uh.at[0], us_sem.at[0], ur_sem.at[0], {"tm": next_t})
    u_prev = remote(u.at[0], uh.at[1], us_sem.at[1], ur_sem.at[1], {"tm": prev_t})

    @pl.when(has_down)
    def _():
        for f in order:
            x_down(f).start()

    @pl.when(has_up)
    def _():
        for f in order:
            x_up(f).start()

    u_next.start()
    u_prev.start()

    @pl.when(jnp.logical_not(has_up))
    def _():
        xh[0] = jnp.zeros((F, C, W), BF16)
        gh[0] = jnp.zeros((F, MP, W), BF16)

    @pl.when(jnp.logical_not(has_down))
    def _():
        xh[1] = jnp.zeros((F, C, W), BF16)
        gh[1] = jnp.zeros((F, MP, W), BF16)

    u_next.wait_recv()
    u_prev.wait_recv()
    for f in (0, F - 1):
        ga[f] = mm(tg[...], u_stack(f))

    h_next = remote(hid.at[F], hid.at[0], hs_sem.at[0], hr_sem.at[0], {"tm": next_t})
    h_prev = remote(hid.at[1], hid.at[F + 1], hs_sem.at[1], hr_sem.at[1], {"tm": prev_t})

    def g_down(f):
        return remote(gs.at[f, H - 1, 1], gh.at[0, f], gs_sem.at[0, f], gr_sem.at[0, f], down_dev)

    def g_up(f):
        return remote(gs.at[f, 0, 1], gh.at[1, f], gs_sem.at[1, f], gr_sem.at[1, f], up_dev)

    for f in order:
        @pl.when(has_up)
        def _():
            x_down(f).wait_recv()

        @pl.when(has_down)
        def _():
            x_up(f).wait_recv()

        rows = [xh[0, f]] + [x[f, h] for h in range(H)] + [xh[1, f]]
        xst = lanes([jnp.concatenate(rows[h : h + 3], axis=0) for h in range(H)])
        y = mm(wf[...], xst)
        hs, gsh = [], []
        for h in range(H):
            sl = slice(h * W, (h + 1) * W)
            pre = (
                shifted(y[0:MP, sl], 1) + y[MP : 2 * MP, sl] + shifted(y[2 * MP :, sl], -1)
            )
            sig = 1.0 / (1.0 + jnp.exp(-pre))
            hv = (pre * sig).astype(BF16)
            hid[f + 1, h] = hv
            hs.append(hv)
            gv = ga[f, :, sl] * sig * (1.0 + pre * (1.0 - sig))
            trio = [shifted(gv, j - 1).astype(BF16) for j in range(3)]
            for j in range(3):
                gs[f, h, j] = trio[j]
            gsh.append(jnp.concatenate(trio, axis=0))
        if f == 0:
            h_prev.start()
        if f == F - 1:
            h_next.start()

        @pl.when(has_down)
        def _():
            g_down(f).start()

        @pl.when(has_up)
        def _():
            g_up(f).start()

        acc[:, 0 : 3 * MP] += mm_nt(xst, lanes(gsh))
        acc[:, T0 : T0 + MP] += mm_nt(u_stack(f), lanes(hs))

    for p in range(owners):
        rs_send[p] = (acc[p * rp : (p + 1) * rp] * factor).astype(BF16)

    def rs_copy(d):
        p, dev = peer(d)
        return remote(rs_send.at[lax.rem(p, owners)], rs_recv.at[d - 1], rss_sem.at[d - 1], rsr_sem.at[d - 1], dev)

    def guarded(cond, do):
        if owners == n:
            do()
        else:
            pl.when(cond)(do)

    for d in range(1, n):
        guarded(peer(d)[0] < owners, lambda: rs_copy(d).start())

    own_rows = pl.ds(pl.multiple_of(ch * CS, CS), CS)
    far_rows = pl.ds(pl.multiple_of(oc * CS, CS), CS)
    to2 = jnp.concatenate([to[own_rows, :], to[far_rows, :]], axis=0)

    def o_copy(f):
        return remote(o_send.at[f], o_recv.at[f], os_sem.at[f], or_sem.at[f], {"chan": oc})

    def i_copy(f):
        return remote(i_send.at[f], i_recv.at[f], is_sem.at[f], ir_sem.at[f], {"chan": oc})

    for f in list(range(1, F - 1)) + [0, F - 1]:
        if f == 0:
            h_next.wait_recv()
        if f == F - 1:
            h_prev.wait_recv()
        st = lanes([jnp.concatenate([hid[f + k, h] for k in range(3)], axis=0) for h in range(H)])
        y = mm(to2, st)
        for h in range(H):
            sl = slice(h * W, (h + 1) * W)
            o_own[f, h] = y[:CS, sl]
            o_send[f, h] = y[CS:, sl].astype(BF16)
        o_copy(f).start()

    def ag_copy(d):
        _, dev = peer(d)
        mine = red.at[lax.rem(g, owners)]
        return remote(mine, mine, ags_sem.at[d - 1], agr_sem.at[d - 1], dev)

    def reduce_piece():
        total = acc[pl.ds(pl.multiple_of(lax.rem(g, owners) * rp, 8), rp), :] * factor
        for d in range(1, n):
            rs_copy(d).wait_recv()
            total = total + rs_recv[d - 1].astype(F32)
        red[lax.rem(g, owners)] = total.astype(BF16)
        for d in range(1, n):
            ag_copy(d).start()

    wi2 = jnp.concatenate(
        [wi[i, own_rows, :] for i in range(3)] + [wi[i, far_rows, :] for i in range(3)], axis=0
    )
    for f in range(F):
        if f == F // 2:
            guarded(g < owners, reduce_piece)

        @pl.when(has_up)
        def _():
            g_down(f).wait_recv()

        @pl.when(has_down)
        def _():
            g_up(f).wait_recv()

        halo = []
        for side in range(2):
            gv = gh[side, f].astype(F32)
            halo.append(jnp.concatenate([shifted(gv, j - 1).astype(BF16) for j in range(3)], axis=0))
        body = [jnp.concatenate([gs[f, h, j] for j in range(3)], axis=0) for h in range(H)]
        y = mm(wi2, lanes([halo[0]] + body + [halo[1]]))
        for h in range(H):
            def part(base):
                s = None
                for i in range(3):
                    e = h + 2 - i
                    v = y[base + i * CS : base + (i + 1) * CS, e * W : (e + 1) * W]
                    s = v if s is None else s + v
                return s

            i_own[f, h] = part(0)
            i_send[f, h] = part(3 * CS).astype(BF16)
        i_copy(f).start()

    for f in range(F):
        o_copy(f).wait_recv()
        out[f] = (o_own[f] + o_recv[f].astype(F32)).astype(BF16)
    for f in range(F):
        i_copy(f).wait_recv()
        ig[f] = (i_own[f] + i_recv[f].astype(F32)).astype(BF16)

    for d in range(1, n):
        src = lax.rem(g + n - d, n)

        def arrive():
            dst = red.at[lax.rem(src, owners)]
            remote(dst, dst, ags_sem.at[d - 1], agr_sem.at[d - 1], peer(n - d)[1]).wait_recv()

        guarded(src < owners, arrive)
    total = jnp.concatenate([red[p].astype(F32) for p in range(owners)], axis=0)
    for i in range(3):
        for j in range(3):
            sg[i, j] = total[i * C : (i + 1) * C, j * MP : j * MP + M]
    for k in range(3):
        tgrad[2 - k] = total[k * C : (k + 1) * C, T0 : T0 + M]

    @pl.when(has_down)
    def _():
        for f in range(F):
            x_down(f).wait_send()
            g_down(f).wait_send()

    @pl.when(has_up)
    def _():
        for f in range(F):
            x_up(f).wait_send()
            g_up(f).wait_send()

    u_next.wait_send()
    u_prev.wait_send()
    h_next.wait_send()
    h_prev.wait_send()
    for f in range(F):
        o_copy(f).wait_send()
        i_copy(f).wait_send()
    for d in range(1, n):
        guarded(peer(d)[0] < owners, lambda: rs_copy(d).wait_send())
        guarded(g < owners, lambda: ag_copy(d).wait_send())


T0 = 256


def shards(x, sw, tw, u):
    F, H, C, W = x.shape
    M = tw.shape[1]
    MP = -(-M // 16) * 16
    T, A = lax.axis_size("tm"), lax.axis_size("axial")
    n = T * A
    factor = 1.0 / math.sqrt(F * T * H * A * W)
    R, L = 3 * C, T0 + 128
    rp = next(r for r in range(8, R + 1, 8) if R % r == 0 and R // r <= n)
    owners = R // rp
    CS = C // 2
    vm = pl.BlockSpec(memory_space=pltpu.VMEM)
    dma = pltpu.SemaphoreType.DMA
    out, ig, sgrad, tgrad = pl.pallas_call(
        functools.partial(kernel, (F, H, C, W, M, MP, T, A, factor, owners, rp)),
        out_shape=(
            jax.ShapeDtypeStruct((F, H, CS, W), BF16),
            jax.ShapeDtypeStruct((F, H, CS, W), BF16),
            jax.ShapeDtypeStruct((3, 3, C, M), F32),
            jax.ShapeDtypeStruct((3, C, M), F32),
        ),
        in_specs=[vm] * 4,
        out_specs=[vm] * 4,
        scratch_shapes=[
            pltpu.VMEM((3 * MP, 3 * C), BF16),
            pltpu.VMEM((3, C, 3 * MP), BF16),
            pltpu.VMEM((MP, 3 * C), BF16),
            pltpu.VMEM((C, 3 * MP), BF16),
            pltpu.VMEM((2, F, C, W), BF16),
            pltpu.VMEM((2, H, C, W), BF16),
            pltpu.VMEM((F + 2, H, MP, W), BF16),
            pltpu.VMEM((F, H, 3, MP, W), BF16),
            pltpu.VMEM((2, F, MP, W), BF16),
            pltpu.VMEM((F, MP, H * W), F32),
            pltpu.VMEM((F, H, CS, W), F32),
            pltpu.VMEM((F, H, CS, W), BF16),
            pltpu.VMEM((F, H, CS, W), BF16),
            pltpu.VMEM((F, H, CS, W), F32),
            pltpu.VMEM((F, H, CS, W), BF16),
            pltpu.VMEM((F, H, CS, W), BF16),
            pltpu.VMEM((R, L), F32),
            pltpu.VMEM((owners, rp, L), BF16),
            pltpu.VMEM((n - 1, rp, L), BF16),
            pltpu.VMEM((owners, rp, L), BF16),
            dma((2, F)), dma((2, F)), dma((2,)), dma((2,)), dma((2,)), dma((2,)),
            dma((2, F)), dma((2, F)),
            dma((F,)), dma((F,)), dma((F,)), dma((F,)),
            dma((n - 1,)), dma((n - 1,)), dma((n - 1,)), dma((n - 1,)),
        ],
        compiler_params=pltpu.CompilerParams(collective_id=0, has_side_effects=True),
    )(x, u, sw, jnp.transpose(tw, (0, 2, 1)))
    return out, ig, sgrad, jnp.transpose(tgrad, (0, 2, 1))


def solution(mesh):
    placed = (
        P(("parts", "tm"), "axial", None, None),
        P("parts", None, None, "chan"),
        P("parts", "chan", None),
        P(("parts", "tm"), "axial", None, None),
    )
    return jax.shard_map(
        shards,
        mesh=mesh,
        in_specs=placed,
        out_specs=(
            P(("parts", "tm"), "axial", "chan", None),
            P(("parts", "tm"), "axial", "chan", None),
            P("parts", None, None, "chan"),
            P("parts", "chan", None),
        ),
        check_vma=False,
    )
```

```python
import functools
import math

import jax
import jax.numpy as jnp
from jax import lax
from jax.experimental import pallas as pl
from jax.experimental.pallas import tpu as pltpu
from jax.sharding import PartitionSpec as P

MESH = pl.DeviceIdType.MESH
F32 = jnp.float32
BF16 = jnp.bfloat16
NT = (((1,), (1,)), ((), ()))


def mm(a, b):
    return jnp.dot(a, b, preferred_element_type=F32)


def mm_nt(a, b):
    return lax.dot_general(a, b, NT, preferred_element_type=F32)


def shifted(block, step):
    if step == 0:
        return block
    width = block.shape[1]
    lane = lax.broadcasted_iota(jnp.int32, block.shape, 1)
    edge = 0 if step > 0 else width - 1
    return jnp.where(lane == edge, 0.0, pltpu.roll(block, step % width, axis=1))


def kernel(
    dims, x_in, u_in, sw_in, tw_in, out, ig, sg, tgrad,
    x, u, sw, tw, load_sem,
    wf, wi, tg, to,
    xh, uh, hid, gs, gh, ga, o_own, o_send, o_recv, i_own, i_send, i_recv,
    acc, rs_send, rs_recv, red,
    xs_sem, xr_sem, us_sem, ur_sem, hs_sem, hr_sem, gs_sem, gr_sem,
    os_sem, or_sem, is_sem, ir_sem, rss_sem, rsr_sem, ags_sem, agr_sem,
):
    F, H, C, W, M, MP, T, A, factor, owners, rp = dims
    CS = C // 2
    n = T * A
    t, a, ch = lax.axis_index("tm"), lax.axis_index("axial"), lax.axis_index("chan")
    oc = 1 - ch
    g = t * A + a
    prev_t, next_t = lax.rem(t + T - 1, T), lax.rem(t + 1, T)

    def peer(d):
        p = lax.rem(g + d, n)
        return p, {"tm": p // A, "axial": lax.rem(p, A)}

    def lanes(rows):
        return jnp.concatenate(rows, axis=1)

    def u_at(f, h):
        if f < 0:
            return uh[0, h]
        if f >= F:
            return uh[1, h]
        return u[f, h]

    def u_stack(f):
        return lanes([jnp.concatenate([u_at(f - 1, h), u_at(f, h), u_at(f + 1, h)], axis=0) for h in range(H)])

    def ga_inner():
        for f in range(1, F - 1):
            ga[f] = mm(tg[...], u_stack(f))

    barrier = pltpu.get_barrier_semaphore()
    for d in range(1, n):
        pl.semaphore_signal(barrier, inc=1, device_id=peer(d)[1], device_id_type=MESH)
    pl.semaphore_signal(barrier, inc=1, device_id={"chan": oc}, device_id_type=MESH)
    loads = [
        pltpu.make_async_copy(src, dst, load_sem.at[k])
        for k, (src, dst) in enumerate(((tw_in, tw), (u_in, u), (sw_in, sw), (x_in, x)))
    ]
    for load in loads:
        load.start()
    acc[...] = jnp.zeros_like(acc)

    def widen(parts):
        zero = jnp.zeros((parts[0].shape[0], MP - M), F32)
        return jnp.concatenate([v for p in parts for v in (p.astype(F32), zero)], axis=1)

    loads[0].wait()
    tcol = [widen([tw[k]]) for k in range(3)]
    tg[...] = jnp.transpose(jnp.concatenate(tcol[::-1], axis=0)).astype(BF16)
    to[...] = jnp.concatenate(tcol, axis=1).astype(BF16)
    loads[1].wait()
    ga_inner()
    loads[2].wait()
    wide = jnp.concatenate([widen([sw[i, j] for j in range(3)]) for i in range(3)], axis=0)
    wf[...] = jnp.transpose(wide).astype(BF16)
    for i in range(3):
        wi[i] = wide[i * C : (i + 1) * C].astype(BF16)
    loads[3].wait()
    pl.semaphore_wait(barrier, n)

    def remote(src, dst, s, r, dev):
        return pltpu.make_async_remote_copy(
            src_ref=src, dst_ref=dst, send_sem=s, recv_sem=r, device_id=dev, device_id_type=MESH
        )

    up_dev = {"axial": jnp.maximum(a - 1, 0)}
    down_dev = {"axial": jnp.minimum(a + 1, A - 1)}
    has_up, has_down = a > 0, a < A - 1
    def x_down(f):
        return remote(x_in.at[f, H - 1], xh.at[0, f], xs_sem.at[0, f], xr_sem.at[0, f], down_dev)

    def x_up(f):
        return remote(x_in.at[f, 0], xh.at[1, f], xs_sem.at[1, f], xr_sem.at[1, f], up_dev)

    order = [0, F - 1] + list(range(1, F - 1))
    u_next = remote(u_in.at[F - 1], uh.at[0], us_sem.at[0], ur_sem.at[0], {"tm": next_t})
    u_prev = remote(u_in.at[0], uh.at[1], us_sem.at[1], ur_sem.at[1], {"tm": prev_t})

    @pl.when(has_down)
    def _():
        for f in order:
            x_down(f).start()

    @pl.when(has_up)
    def _():
        for f in order:
            x_up(f).start()

    u_next.start()
    u_prev.start()

    @pl.when(jnp.logical_not(has_up))
    def _():
        xh[0] = jnp.zeros((F, C, W), BF16)
        gh[0] = jnp.zeros((F, MP, W), BF16)

    @pl.when(jnp.logical_not(has_down))
    def _():
        xh[1] = jnp.zeros((F, C, W), BF16)
        gh[1] = jnp.zeros((F, MP, W), BF16)

    u_next.wait_recv()
    u_prev.wait_recv()
    for f in (0, F - 1):
        ga[f] = mm(tg[...], u_stack(f))

    h_next = remote(hid.at[F], hid.at[0], hs_sem.at[0], hr_sem.at[0], {"tm": next_t})
    h_prev = remote(hid.at[1], hid.at[F + 1], hs_sem.at[1], hr_sem.at[1], {"tm": prev_t})

    def g_down(f):
        return remote(gs.at[f, H - 1, 1], gh.at[0, f], gs_sem.at[0, f], gr_sem.at[0, f], down_dev)

    def g_up(f):
        return remote(gs.at[f, 0, 1], gh.at[1, f], gs_sem.at[1, f], gr_sem.at[1, f], up_dev)

    for f in order:
        @pl.when(has_up)
        def _():
            x_down(f).wait_recv()

        @pl.when(has_down)
        def _():
            x_up(f).wait_recv()

        rows = [xh[0, f]] + [x[f, h] for h in range(H)] + [xh[1, f]]
        xst = lanes([jnp.concatenate(rows[h : h + 3], axis=0) for h in range(H)])
        y = mm(wf[...], xst)
        hs, gsh = [], []
        for h in range(H):
            sl = slice(h * W, (h + 1) * W)
            pre = (
                shifted(y[0:MP, sl], 1) + y[MP : 2 * MP, sl] + shifted(y[2 * MP :, sl], -1)
            )
            sig = 1.0 / (1.0 + jnp.exp(-pre))
            hv = (pre * sig).astype(BF16)
            hid[f + 1, h] = hv
            hs.append(hv)
            gv = ga[f, :, sl] * sig * (1.0 + pre * (1.0 - sig))
            trio = [shifted(gv, j - 1).astype(BF16) for j in range(3)]
            for j in range(3):
                gs[f, h, j] = trio[j]
            gsh.append(jnp.concatenate(trio, axis=0))
        if f == 0:
            h_prev.start()
        if f == F - 1:
            h_next.start()

        @pl.when(has_down)
        def _():
            g_down(f).start()

        @pl.when(has_up)
        def _():
            g_up(f).start()

        acc[:, 0 : 3 * MP] += mm_nt(xst, lanes(gsh))
        acc[:, T0 : T0 + MP] += mm_nt(u_stack(f), lanes(hs))

    for p in range(owners):
        rs_send[p] = (acc[p * rp : (p + 1) * rp] * factor).astype(BF16)

    def rs_copy(d):
        p, dev = peer(d)
        return remote(rs_send.at[lax.rem(p, owners)], rs_recv.at[d - 1], rss_sem.at[d - 1], rsr_sem.at[d - 1], dev)

    def guarded(cond, do):
        if owners == n:
            do()
        else:
            pl.when(cond)(do)

    for d in range(1, n):
        guarded(peer(d)[0] < owners, lambda: rs_copy(d).start())

    own_rows = pl.ds(pl.multiple_of(ch * CS, CS), CS)
    far_rows = pl.ds(pl.multiple_of(oc * CS, CS), CS)
    to2 = jnp.concatenate([to[own_rows, :], to[far_rows, :]], axis=0)

    def o_copy(f):
        return remote(o_send.at[f], o_recv.at[f], os_sem.at[f], or_sem.at[f], {"chan": oc})

    def i_copy(f):
        return remote(i_send.at[f], i_recv.at[f], is_sem.at[f], ir_sem.at[f], {"chan": oc})

    for f in list(range(1, F - 1)) + [0, F - 1]:
        if f == 0:
            h_next.wait_recv()
        if f == F - 1:
            h_prev.wait_recv()
        st = lanes([jnp.concatenate([hid[f + k, h] for k in range(3)], axis=0) for h in range(H)])
        y = mm(to2, st)
        for h in range(H):
            sl = slice(h * W, (h + 1) * W)
            o_own[f, h] = y[:CS, sl]
            o_send[f, h] = y[CS:, sl].astype(BF16)
        o_copy(f).start()

    def ag_copy(d):
        _, dev = peer(d)
        mine = red.at[lax.rem(g, owners)]
        return remote(mine, mine, ags_sem.at[d - 1], agr_sem.at[d - 1], dev)

    def reduce_piece():
        total = acc[pl.ds(pl.multiple_of(lax.rem(g, owners) * rp, 8), rp), :] * factor
        for d in range(1, n):
            rs_copy(d).wait_recv()
            total = total + rs_recv[d - 1].astype(F32)
        red[lax.rem(g, owners)] = total.astype(BF16)
        for d in range(1, n):
            ag_copy(d).start()

    wi2 = jnp.concatenate(
        [wi[i, own_rows, :] for i in range(3)] + [wi[i, far_rows, :] for i in range(3)], axis=0
    )
    for f in range(F):
        if f == F // 2:
            guarded(g < owners, reduce_piece)

        @pl.when(has_up)
        def _():
            g_down(f).wait_recv()

        @pl.when(has_down)
        def _():
            g_up(f).wait_recv()

        halo = []
        for side in range(2):
            gv = gh[side, f].astype(F32)
            halo.append(jnp.concatenate([shifted(gv, j - 1).astype(BF16) for j in range(3)], axis=0))
        body = [jnp.concatenate([gs[f, h, j] for j in range(3)], axis=0) for h in range(H)]
        y = mm(wi2, lanes([halo[0]] + body + [halo[1]]))
        for h in range(H):
            def part(base):
                s = None
                for i in range(3):
                    e = h + 2 - i
                    v = y[base + i * CS : base + (i + 1) * CS, e * W : (e + 1) * W]
                    s = v if s is None else s + v
                return s

            i_own[f, h] = part(0)
            i_send[f, h] = part(3 * CS).astype(BF16)
        i_copy(f).start()

    for f in range(F):
        o_copy(f).wait_recv()
        out[f] = (o_own[f] + o_recv[f].astype(F32)).astype(BF16)
    for f in range(F):
        i_copy(f).wait_recv()
        ig[f] = (i_own[f] + i_recv[f].astype(F32)).astype(BF16)

    for d in range(1, n):
        src = lax.rem(g + n - d, n)

        def arrive():
            dst = red.at[lax.rem(src, owners)]
            remote(dst, dst, ags_sem.at[d - 1], agr_sem.at[d - 1], peer(n - d)[1]).wait_recv()

        guarded(src < owners, arrive)
    total = jnp.concatenate([red[p].astype(F32) for p in range(owners)], axis=0)
    for i in range(3):
        for j in range(3):
            sg[i, j] = total[i * C : (i + 1) * C, j * MP : j * MP + M]
    for k in range(3):
        tgrad[2 - k] = total[k * C : (k + 1) * C, T0 : T0 + M]

    @pl.when(has_down)
    def _():
        for f in range(F):
            x_down(f).wait_send()
            g_down(f).wait_send()

    @pl.when(has_up)
    def _():
        for f in range(F):
            x_up(f).wait_send()
            g_up(f).wait_send()

    u_next.wait_send()
    u_prev.wait_send()
    h_next.wait_send()
    h_prev.wait_send()
    for f in range(F):
        o_copy(f).wait_send()
        i_copy(f).wait_send()
    for d in range(1, n):
        guarded(peer(d)[0] < owners, lambda: rs_copy(d).wait_send())
        guarded(g < owners, lambda: ag_copy(d).wait_send())


T0 = 256
VMEM_BYTES = 24 * 1024 * 1024


def store_kernel(*refs):
    sems = refs[8]
    copies = [pltpu.make_async_copy(refs[k], refs[4 + k], sems.at[k]) for k in range(4)]
    for copy in copies:
        copy.start()
    for copy in copies:
        copy.wait()


def shards(x, sw, tw, u):
    F, H, C, W = x.shape
    M = tw.shape[1]
    MP = -(-M // 16) * 16
    T, A = lax.axis_size("tm"), lax.axis_size("axial")
    n = T * A
    factor = 1.0 / math.sqrt(F * T * H * A * W)
    R, L = 3 * C, T0 + 128
    rp = next(r for r in range(8, R + 1, 8) if R % r == 0 and R // r <= n)
    owners = R // rp
    CS = C // 2
    vm = pl.BlockSpec(memory_space=pltpu.VMEM)
    hbm = pl.BlockSpec(memory_space=pltpu.HBM)
    dma = pltpu.SemaphoreType.DMA
    results = pl.pallas_call(
        functools.partial(kernel, (F, H, C, W, M, MP, T, A, factor, owners, rp)),
        out_shape=(
            pltpu.VMEM((F, H, CS, W), BF16),
            pltpu.VMEM((F, H, CS, W), BF16),
            pltpu.VMEM((3, 3, C, M), F32),
            pltpu.VMEM((3, C, M), F32),
        ),
        in_specs=[hbm] * 4,
        out_specs=[vm] * 4,
        scratch_shapes=[
            pltpu.VMEM((F, H, C, W), BF16),
            pltpu.VMEM((F, H, C, W), BF16),
            pltpu.VMEM((3, 3, C, M), BF16),
            pltpu.VMEM((3, C, M), BF16),
            dma((4,)),
            pltpu.VMEM((3 * MP, 3 * C), BF16),
            pltpu.VMEM((3, C, 3 * MP), BF16),
            pltpu.VMEM((MP, 3 * C), BF16),
            pltpu.VMEM((C, 3 * MP), BF16),
            pltpu.VMEM((2, F, C, W), BF16),
            pltpu.VMEM((2, H, C, W), BF16),
            pltpu.VMEM((F + 2, H, MP, W), BF16),
            pltpu.VMEM((F, H, 3, MP, W), BF16),
            pltpu.VMEM((2, F, MP, W), BF16),
            pltpu.VMEM((F, MP, H * W), F32),
            pltpu.VMEM((F, H, CS, W), F32),
            pltpu.VMEM((F, H, CS, W), BF16),
            pltpu.VMEM((F, H, CS, W), BF16),
            pltpu.VMEM((F, H, CS, W), F32),
            pltpu.VMEM((F, H, CS, W), BF16),
            pltpu.VMEM((F, H, CS, W), BF16),
            pltpu.VMEM((R, L), F32),
            pltpu.VMEM((owners, rp, L), BF16),
            pltpu.VMEM((n - 1, rp, L), BF16),
            pltpu.VMEM((owners, rp, L), BF16),
            dma((2, F)), dma((2, F)), dma((2,)), dma((2,)), dma((2,)), dma((2,)),
            dma((2, F)), dma((2, F)),
            dma((F,)), dma((F,)), dma((F,)), dma((F,)),
            dma((n - 1,)), dma((n - 1,)), dma((n - 1,)), dma((n - 1,)),
        ],
        compiler_params=pltpu.CompilerParams(collective_id=0, has_side_effects=True, vmem_limit_bytes=VMEM_BYTES),
    )(*(pltpu.with_memory_space_constraint(v, pltpu.HBM) for v in (x, u, sw, jnp.transpose(tw, (0, 2, 1)))))
    out, ig, sgrad, tgrad = pl.pallas_call(
        store_kernel,
        out_shape=[jax.ShapeDtypeStruct(r.shape, r.dtype) for r in results],
        in_specs=[vm] * 4,
        out_specs=[hbm] * 4,
        scratch_shapes=[dma((4,))],
        compiler_params=pltpu.CompilerParams(vmem_limit_bytes=VMEM_BYTES),
    )(*results)
    return out, ig, sgrad, jnp.transpose(tgrad, (0, 2, 1))


def solution(mesh):
    placed = (
        P(("parts", "tm"), "axial", None, None),
        P("parts", None, None, "chan"),
        P("parts", "chan", None),
        P(("parts", "tm"), "axial", None, None),
    )
    return jax.shard_map(
        shards,
        mesh=mesh,
        in_specs=placed,
        out_specs=(
            P(("parts", "tm"), "axial", "chan", None),
            P(("parts", "tm"), "axial", "chan", None),
            P("parts", None, None, "chan"),
            P("parts", "chan", None),
        ),
        check_vma=False,
    )
```

```python
import functools
import math

import jax
import jax.numpy as jnp
from jax import lax
from jax.experimental import pallas as pl
from jax.experimental.pallas import tpu as pltpu
from jax.sharding import PartitionSpec as P

MESH = pl.DeviceIdType.MESH
F32 = jnp.float32
BF16 = jnp.bfloat16
NT = (((1,), (1,)), ((), ()))


def mm(a, b):
    return jnp.dot(a, b, preferred_element_type=F32)


def mm_nt(a, b):
    return lax.dot_general(a, b, NT, preferred_element_type=F32)


def shifted(block, step):
    if step == 0:
        return block
    width = block.shape[1]
    lane = lax.broadcasted_iota(jnp.int32, block.shape, 1)
    edge = 0 if step > 0 else width - 1
    return jnp.where(lane == edge, 0.0, pltpu.roll(block, step % width, axis=1))


def kernel(
    dims, x_in, u_in, sw_in, tw_in, out, ig, sg, tgrad,
    x, u, sw, tw, load_sem,
    wf, wi, tg, to,
    xh, uh, hid, gs, gh, ga, o_own, o_send, o_recv, i_own, i_send, i_recv,
    acc, packed, rs_send, rs_recv, red,
    xs_sem, xr_sem, us_sem, ur_sem, hs_sem, hr_sem, gs_sem, gr_sem,
    os_sem, or_sem, is_sem, ir_sem, rss_sem, rsr_sem, ags_sem, agr_sem,
):
    F, H, C, W, M, MP, T, A, factor, owners, rp = dims
    CS = C // 2
    n = T * A
    FR, LW = 3 * C // 4, 4 * M - 256
    nb = -(-FR // (8 * owners))
    t, a, ch = lax.axis_index("tm"), lax.axis_index("axial"), lax.axis_index("chan")
    oc = 1 - ch
    g = t * A + a
    prev_t, next_t = lax.rem(t + T - 1, T), lax.rem(t + 1, T)

    def peer(d):
        p = lax.rem(g + d, n)
        return p, {"tm": p // A, "axial": lax.rem(p, A)}

    def lanes(rows):
        return jnp.concatenate(rows, axis=1)

    def u_at(f, h):
        if f < 0:
            return uh[0, h]
        if f >= F:
            return uh[1, h]
        return u[f, h]

    def u_stack(f):
        return lanes([jnp.concatenate([u_at(f - 1, h), u_at(f, h), u_at(f + 1, h)], axis=0) for h in range(H)])

    def ga_inner():
        for f in range(1, F - 1):
            ga[f] = mm(tg[...], u_stack(f))

    barrier = pltpu.get_barrier_semaphore()
    for d in range(1, n):
        pl.semaphore_signal(barrier, inc=1, device_id=peer(d)[1], device_id_type=MESH)
    pl.semaphore_signal(barrier, inc=1, device_id={"chan": oc}, device_id_type=MESH)
    loads = [
        pltpu.make_async_copy(src, dst, load_sem.at[k])
        for k, (src, dst) in enumerate(((tw_in, tw), (u_in, u), (sw_in, sw), (x_in, x)))
    ]
    for load in loads:
        load.start()
    acc[...] = jnp.zeros_like(acc)

    def widen(parts):
        zero = jnp.zeros((parts[0].shape[0], MP - M), F32)
        return jnp.concatenate([v for p in parts for v in (p.astype(F32), zero)], axis=1)

    loads[0].wait()
    tcol = [widen([tw[k]]) for k in range(3)]
    tg[...] = jnp.transpose(jnp.concatenate(tcol[::-1], axis=0)).astype(BF16)
    to[...] = jnp.concatenate(tcol, axis=1).astype(BF16)
    loads[1].wait()
    ga_inner()
    loads[2].wait()
    wide = jnp.concatenate([widen([sw[i, j] for j in range(3)]) for i in range(3)], axis=0)
    wf[...] = jnp.transpose(wide).astype(BF16)
    for i in range(3):
        wi[i] = wide[i * C : (i + 1) * C].astype(BF16)
    loads[3].wait()
    pl.semaphore_wait(barrier, n)

    def remote(src, dst, s, r, dev):
        return pltpu.make_async_remote_copy(
            src_ref=src, dst_ref=dst, send_sem=s, recv_sem=r, device_id=dev, device_id_type=MESH
        )

    up_dev = {"axial": jnp.maximum(a - 1, 0)}
    down_dev = {"axial": jnp.minimum(a + 1, A - 1)}
    has_up, has_down = a > 0, a < A - 1
    def x_down(f):
        return remote(x_in.at[f, H - 1], xh.at[0, f], xs_sem.at[0, f], xr_sem.at[0, f], down_dev)

    def x_up(f):
        return remote(x_in.at[f, 0], xh.at[1, f], xs_sem.at[1, f], xr_sem.at[1, f], up_dev)

    inner = list(range(1, F - 1))
    order = inner[: len(inner) // 2] + [0, F - 1] + inner[len(inner) // 2 :]
    u_next = remote(u_in.at[F - 1], uh.at[0], us_sem.at[0], ur_sem.at[0], {"tm": next_t})
    u_prev = remote(u_in.at[0], uh.at[1], us_sem.at[1], ur_sem.at[1], {"tm": prev_t})

    @pl.when(has_down)
    def _():
        for f in order:
            x_down(f).start()

    @pl.when(has_up)
    def _():
        for f in order:
            x_up(f).start()

    u_next.start()
    u_prev.start()

    @pl.when(jnp.logical_not(has_up))
    def _():
        xh[0] = jnp.zeros((F, C, W), BF16)
        gh[0] = jnp.zeros((F, MP, W), BF16)

    @pl.when(jnp.logical_not(has_down))
    def _():
        xh[1] = jnp.zeros((F, C, W), BF16)
        gh[1] = jnp.zeros((F, MP, W), BF16)

    h_next = remote(hid.at[F], hid.at[0], hs_sem.at[0], hr_sem.at[0], {"tm": next_t})
    h_prev = remote(hid.at[1], hid.at[F + 1], hs_sem.at[1], hr_sem.at[1], {"tm": prev_t})

    def g_down(f):
        return remote(gs.at[f, H - 1, 1], gh.at[0, f], gs_sem.at[0, f], gr_sem.at[0, f], down_dev)

    def g_up(f):
        return remote(gs.at[f, 0, 1], gh.at[1, f], gs_sem.at[1, f], gr_sem.at[1, f], up_dev)

    for f in order:
        @pl.when(has_up)
        def _():
            x_down(f).wait_recv()

        @pl.when(has_down)
        def _():
            x_up(f).wait_recv()

        if f == 0:
            u_next.wait_recv()
            u_prev.wait_recv()
        if f in (0, F - 1):
            ga[f] = mm(tg[...], u_stack(f))
        rows = [xh[0, f]] + [x[f, h] for h in range(H)] + [xh[1, f]]
        xst = lanes([jnp.concatenate(rows[h : h + 3], axis=0) for h in range(H)])
        y = mm(wf[...], xst)
        hs, gsh = [], []
        for h in range(H):
            sl = slice(h * W, (h + 1) * W)
            pre = (
                shifted(y[0:MP, sl], 1) + y[MP : 2 * MP, sl] + shifted(y[2 * MP :, sl], -1)
            )
            sig = 1.0 / (1.0 + jnp.exp(-pre))
            hv = (pre * sig).astype(BF16)
            hid[f + 1, h] = hv
            hs.append(hv)
            gv = ga[f, :, sl] * sig * (1.0 + pre * (1.0 - sig))
            trio = [shifted(gv, j - 1).astype(BF16) for j in range(3)]
            for j in range(3):
                gs[f, h, j] = trio[j]
            gsh.append(jnp.concatenate(trio, axis=0))
        if f == 0:
            h_prev.start()
        if f == F - 1:
            h_next.start()

        @pl.when(has_down)
        def _():
            g_down(f).start()

        @pl.when(has_up)
        def _():
            g_up(f).start()

        acc[:, 0 : 3 * MP] += mm_nt(xst, lanes(gsh))
        acc[:, T0 : T0 + MP] += mm_nt(u_stack(f), lanes(hs))

    dense = jnp.concatenate(
        [acc[:, j * MP : j * MP + M] for j in range(3)] + [acc[:, T0 : T0 + M]], axis=1
    ) * factor
    rest = dense[:, 256:]
    folded = jnp.concatenate([rest[q * FR : (q + 1) * FR] for q in range(4)], axis=1)
    if owners * nb * 8 > FR:
        spare = jnp.zeros((owners * nb * 8 - FR, 128), F32)
        folded = jnp.concatenate([folded, spare], axis=0)
    for p in range(owners):
        block = dense[p * rp : (p + 1) * rp]
        tail = folded[p * nb * 8 : (p + 1) * nb * 8]
        block = jnp.concatenate([block[:, :128], block[:, 128:256], tail], axis=0)
        packed[p] = block
        rs_send[p] = block.astype(BF16)

    def rs_copy(d):
        p, dev = peer(d)
        return remote(rs_send.at[lax.rem(p, owners)], rs_recv.at[d - 1], rss_sem.at[d - 1], rsr_sem.at[d - 1], dev)

    def guarded(cond, do):
        if owners == n:
            do()
        else:
            pl.when(cond)(do)

    for d in range(1, n):
        guarded(peer(d)[0] < owners, lambda: rs_copy(d).start())

    own_rows = pl.ds(pl.multiple_of(ch * CS, CS), CS)
    far_rows = pl.ds(pl.multiple_of(oc * CS, CS), CS)
    to2 = jnp.concatenate([to[own_rows, :], to[far_rows, :]], axis=0)

    def o_copy(f):
        return remote(o_send.at[f], o_recv.at[f], os_sem.at[f], or_sem.at[f], {"chan": oc})

    def i_copy(f):
        return remote(i_send.at[f], i_recv.at[f], is_sem.at[f], ir_sem.at[f], {"chan": oc})

    def output_frame(f):
        st = lanes([jnp.concatenate([hid[f + k, h] for k in range(3)], axis=0) for h in range(H)])
        y = mm(to2, st)
        for h in range(H):
            sl = slice(h * W, (h + 1) * W)
            o_own[f, h] = y[:CS, sl]
            o_send[f, h] = y[CS:, sl].astype(BF16)
        o_copy(f).start()

    for f in inner:
        output_frame(f)

    def ag_copy(d):
        _, dev = peer(d)
        mine = red.at[lax.rem(g, owners)]
        return remote(mine, mine, ags_sem.at[d - 1], agr_sem.at[d - 1], dev)

    def reduce_piece():
        total = packed[lax.rem(g, owners)]
        for d in range(1, n):
            rs_copy(d).wait_recv()
            total = total + rs_recv[d - 1].astype(F32)
        red[lax.rem(g, owners)] = total.astype(BF16)
        for d in range(1, n):
            ag_copy(d).start()

    wi2 = jnp.concatenate(
        [wi[i, own_rows, :] for i in range(3)] + [wi[i, far_rows, :] for i in range(3)], axis=0
    )
    for f in order:
        @pl.when(has_up)
        def _():
            g_down(f).wait_recv()

        @pl.when(has_down)
        def _():
            g_up(f).wait_recv()

        halo = []
        for side in range(2):
            gv = gh[side, f].astype(F32)
            halo.append(jnp.concatenate([shifted(gv, j - 1).astype(BF16) for j in range(3)], axis=0))
        body = [jnp.concatenate([gs[f, h, j] for j in range(3)], axis=0) for h in range(H)]
        y = mm(wi2, lanes([halo[0]] + body + [halo[1]]))
        for h in range(H):
            def part(base):
                s = None
                for i in range(3):
                    e = h + 2 - i
                    v = y[base + i * CS : base + (i + 1) * CS, e * W : (e + 1) * W]
                    s = v if s is None else s + v
                return s

            i_own[f, h] = part(0)
            i_send[f, h] = part(3 * CS).astype(BF16)
        i_copy(f).start()

    guarded(g < owners, reduce_piece)
    h_next.wait_recv()
    output_frame(0)
    h_prev.wait_recv()
    output_frame(F - 1)
    for f in range(F):
        o_copy(f).wait_recv()
        out[f] = (o_own[f] + o_recv[f].astype(F32)).astype(BF16)
    for f in range(F):
        i_copy(f).wait_recv()
        ig[f] = (i_own[f] + i_recv[f].astype(F32)).astype(BF16)

    for d in range(1, n):
        src = lax.rem(g + n - d, n)

        def arrive():
            dst = red.at[lax.rem(src, owners)]
            remote(dst, dst, ags_sem.at[d - 1], agr_sem.at[d - 1], peer(n - d)[1]).wait_recv()

        guarded(src < owners, arrive)
    got = [red[p].astype(F32) for p in range(owners)]
    tails = jnp.concatenate([v[2 * rp :] for v in got], axis=0)[:FR]
    total = jnp.concatenate(
        [
            jnp.concatenate([v[:rp] for v in got], axis=0),
            jnp.concatenate([v[rp : 2 * rp] for v in got], axis=0),
            jnp.concatenate([tails[:, q * LW : (q + 1) * LW] for q in range(4)], axis=0),
        ],
        axis=1,
    )
    for i in range(3):
        for j in range(3):
            sg[i, j] = total[i * C : (i + 1) * C, j * M : (j + 1) * M]
    for k in range(3):
        tgrad[2 - k] = total[k * C : (k + 1) * C, 3 * M :]

    @pl.when(has_down)
    def _():
        for f in range(F):
            x_down(f).wait_send()
            g_down(f).wait_send()

    @pl.when(has_up)
    def _():
        for f in range(F):
            x_up(f).wait_send()
            g_up(f).wait_send()

    u_next.wait_send()
    u_prev.wait_send()
    h_next.wait_send()
    h_prev.wait_send()
    for f in range(F):
        o_copy(f).wait_send()
        i_copy(f).wait_send()
    for d in range(1, n):
        guarded(peer(d)[0] < owners, lambda: rs_copy(d).wait_send())
        guarded(g < owners, lambda: ag_copy(d).wait_send())


T0 = 256
VMEM_BYTES = 24 * 1024 * 1024


def store_kernel(*refs):
    sems = refs[8]
    copies = [pltpu.make_async_copy(refs[k], refs[4 + k], sems.at[k]) for k in range(4)]
    for copy in copies:
        copy.start()
    for copy in copies:
        copy.wait()


def shards(x, sw, tw, u):
    F, H, C, W = x.shape
    M = tw.shape[1]
    MP = -(-M // 16) * 16
    T, A = lax.axis_size("tm"), lax.axis_size("axial")
    n = T * A
    factor = 1.0 / math.sqrt(F * T * H * A * W)
    R, L = 3 * C, T0 + 128
    rp = next(r for r in range(8, R + 1, 8) if R % r == 0 and R // r <= n)
    owners = R // rp
    PR = 2 * rp + 8 * -(-R // (32 * owners))
    CS = C // 2
    vm = pl.BlockSpec(memory_space=pltpu.VMEM)
    hbm = pl.BlockSpec(memory_space=pltpu.HBM)
    dma = pltpu.SemaphoreType.DMA
    results = pl.pallas_call(
        functools.partial(kernel, (F, H, C, W, M, MP, T, A, factor, owners, rp)),
        out_shape=(
            pltpu.VMEM((F, H, CS, W), BF16),
            pltpu.VMEM((F, H, CS, W), BF16),
            pltpu.VMEM((3, 3, C, M), F32),
            pltpu.VMEM((3, C, M), F32),
        ),
        in_specs=[hbm] * 4,
        out_specs=[vm] * 4,
        scratch_shapes=[
            pltpu.VMEM((F, H, C, W), BF16),
            pltpu.VMEM((F, H, C, W), BF16),
            pltpu.VMEM((3, 3, C, M), BF16),
            pltpu.VMEM((3, C, M), BF16),
            dma((4,)),
            pltpu.VMEM((3 * MP, 3 * C), BF16),
            pltpu.VMEM((3, C, 3 * MP), BF16),
            pltpu.VMEM((MP, 3 * C), BF16),
            pltpu.VMEM((C, 3 * MP), BF16),
            pltpu.VMEM((2, F, C, W), BF16),
            pltpu.VMEM((2, H, C, W), BF16),
            pltpu.VMEM((F + 2, H, MP, W), BF16),
            pltpu.VMEM((F, H, 3, MP, W), BF16),
            pltpu.VMEM((2, F, MP, W), BF16),
            pltpu.VMEM((F, MP, H * W), F32),
            pltpu.VMEM((F, H, CS, W), F32),
            pltpu.VMEM((F, H, CS, W), BF16),
            pltpu.VMEM((F, H, CS, W), BF16),
            pltpu.VMEM((F, H, CS, W), F32),
            pltpu.VMEM((F, H, CS, W), BF16),
            pltpu.VMEM((F, H, CS, W), BF16),
            pltpu.VMEM((R, L), F32),
            pltpu.VMEM((owners, PR, 128), F32),
            pltpu.VMEM((owners, PR, 128), BF16),
            pltpu.VMEM((n - 1, PR, 128), BF16),
            pltpu.VMEM((owners, PR, 128), BF16),
            dma((2, F)), dma((2, F)), dma((2,)), dma((2,)), dma((2,)), dma((2,)),
            dma((2, F)), dma((2, F)),
            dma((F,)), dma((F,)), dma((F,)), dma((F,)),
            dma((n - 1,)), dma((n - 1,)), dma((n - 1,)), dma((n - 1,)),
        ],
        compiler_params=pltpu.CompilerParams(collective_id=0, has_side_effects=True, vmem_limit_bytes=VMEM_BYTES),
    )(*(pltpu.with_memory_space_constraint(v, pltpu.HBM) for v in (x, u, sw, jnp.transpose(tw, (0, 2, 1)))))
    out, ig, sgrad, tgrad = pl.pallas_call(
        store_kernel,
        out_shape=[jax.ShapeDtypeStruct(r.shape, r.dtype) for r in results],
        in_specs=[vm] * 4,
        out_specs=[hbm] * 4,
        scratch_shapes=[dma((4,))],
        compiler_params=pltpu.CompilerParams(vmem_limit_bytes=VMEM_BYTES),
    )(*results)
    return out, ig, sgrad, jnp.transpose(tgrad, (0, 2, 1))


def solution(mesh):
    placed = (
        P(("parts", "tm"), "axial", None, None),
        P("parts", None, None, "chan"),
        P("parts", "chan", None),
        P(("parts", "tm"), "axial", None, None),
    )
    return jax.shard_map(
        shards,
        mesh=mesh,
        in_specs=placed,
        out_specs=(
            P(("parts", "tm"), "axial", "chan", None),
            P(("parts", "tm"), "axial", "chan", None),
            P("parts", None, None, "chan"),
            P("parts", "chan", None),
        ),
        check_vma=False,
    )
```
